32 devices in a mesh: ctx: 8 (over z, x), head: 4 (over y, core).
Axes of the slice: x: 2, y: 2, z: 4, core: 2. Of those that a mesh axis runs over, the one named last changes fastest.
Arguments:
- q_nope: bfloat16 [1024, 4096], P('ctx', 'head'), may hold values from -6 to 6
- q_rope: bfloat16 [1024, 2048], P('ctx', 'head'), may hold values from -300 to 300
- latent: bfloat16 [1024, 512], P('ctx'), may hold values from -6 to 6
- k_rope: bfloat16 [1024, 64], P('ctx'), may hold values from -4 to 4
- span_order: int32 [16], replicated, may hold values from 0 to 15, each once
- w_uk: bfloat16 [512, 4096], P(None, 'head'), may hold values from -0.25 to 0.25
- w_uv: bfloat16 [512, 4096], P(None, 'head'), may hold values from -0.25 to 0.25
- w_o: bfloat16 [4096, 7168], P('head', 'ctx'), may hold values from -0.125 to 0.125
Outputs:
- attended: bfloat16 [1024, 7168], P('ctx', 'head')
The draws below stay inside these ranges and needn't reach their ends.
Inputs may be any that keep to these rules, and one draw needn't show every extreme that they name: `span_order`: a permutation of 0 to 15.
All inputs are finite; a program needn't handle non-finite values.
Results may differ from the reference program's by a relative error of at most 0.014.
Values may be sent and summed in bfloat16 or wider, within the bound.
No kernel may reach another device: no remote copies, remote signals or barrier semaphores. Data moves between devices by JAX's collectives and lax.ppermute only.
A program may use at most 128 MiB of HBM per device.

```python
import math
import jax
import jax.numpy as jnp
from jax import lax

D = 7168
LAT = 512
ROPE = 64
NOPE = 128
VDIM = 128
HEAD_DEV = 8
TOK_DEV = 128
HEADS = 32
TOKENS = 1024
SPANS = 16
N_HEAD = 4


def rope_pair(key):
    keys_rot = jnp.clip(jax.random.normal(jax.random.fold_in(key, 11), (TOKENS, ROPE), jnp.float32), -4.0, 4.0)
    query_rot = jnp.clip(jax.random.normal(jax.random.fold_in(key, 12), (TOKENS, HEADS * ROPE), jnp.float32), -4.0, 4.0)
    return (query_rot, keys_rot)


def draw_q_rope(key, part):
    return rope_pair(key)[0].astype(jnp.bfloat16)


def draw_k_rope(key, part):
    return rope_pair(key)[1].astype(jnp.bfloat16)


def raised(entries, stream_key, source, target, blocks, factor):
    def block_of(dim):
        return (jnp.arange(entries.shape[dim]) // (entries.shape[dim] // blocks)).reshape((-1,) + (1,) * (entries.ndim - 1 - dim))

    near = jax.random.permutation(stream_key, blocks)[block_of(target)]
    far = (block_of(target) + blocks // 2) % blocks
    return jnp.where((block_of(source) == near) | (block_of(source) == far), factor * entries, entries)


def steps_of(own_key, shape, cuts, low, largest):
    def one(position, parts):
        heights = jax.random.uniform(jax.random.fold_in(jax.random.fold_in(own_key, 6), position), (parts,), jnp.float32, low / len(cuts), largest / len(cuts))
        return jnp.repeat(jnp.exp(heights), shape[position] // parts).reshape((-1,) + (1,) * (len(shape) - position - 1))

    gain = one(*cuts[0])
    for cut in cuts[1:]:
        gain = gain * one(*cut)
    return gain


def scatter_about(key, extent, spread, limit, cuts=(), kind=jnp.bfloat16):
    gain = steps_of(key, extent, cuts, -0.22, 0.18) if cuts else 1.0
    result = jax.random.normal(key, extent, jnp.float32) * spread * gain
    return jnp.minimum(jnp.maximum(result, -limit), limit).astype(kind)


def noise_with(rng, dims, scale, most, shards, heavy, held_as=jnp.bfloat16):
    array = scale * jax.random.normal(rng, dims, jnp.float32)
    if shards:
        array = array * steps_of(rng, dims, shards, -0.22, 0.18)
    return jnp.clip(raised(array, jax.random.fold_in(rng, 3), *heavy), -most, most).astype(held_as)


def setup_inputs(seed: int = 0) -> dict:
    key_list = jax.random.split(jax.random.key(seed), 9)
    return {
        "q_nope": scatter_about(key_list[0], (TOKENS, HEADS * NOPE), 1.0, 6.0, ((0, 8), (1, 4))),
        "q_rope": draw_q_rope(jax.random.fold_in(key_list[8], 71), 0),
        "latent": scatter_about(key_list[2], (TOKENS, LAT), 1.0, 6.0, ((0, 8),)),
        "k_rope": draw_k_rope(jax.random.fold_in(key_list[8], 71), 0),
        "span_order": jax.random.permutation(key_list[4], SPANS).astype(jnp.int32),
        "w_uk": scatter_about(key_list[5], (LAT, HEADS * NOPE), LAT ** -0.5, 0.25, ((1, 4),)),
        "w_uv": scatter_about(key_list[6], (LAT, HEADS * VDIM), LAT ** -0.5, 0.25, ((1, 4),)),
        "w_o": noise_with(key_list[7], (HEADS * VDIM, D), (HEADS * VDIM) ** -0.5, 0.125, ((0, 4), (1, 8)), (0, 1, 8, 2.0)),
    }


def reference(q_nope, q_rope, latent, k_rope, span_order, w_uk, w_uv, w_o):
    half = TOK_DEV // 2
    heads = HEADS
    scale = 1.0 / math.sqrt(NOPE + ROPE)
    slot_ids = jnp.arange(SPANS, dtype=jnp.int32)
    slot_of_span = jnp.zeros((SPANS,), jnp.int32).at[span_order].set(slot_ids)
    places = jnp.arange(TOKENS, dtype=jnp.int32)
    row_of = (slot_of_span[places // half] * half + places % half).astype(jnp.int32)
    qn = q_nope[row_of].reshape(TOKENS, heads, NOPE)
    qr = q_rope[row_of].reshape(TOKENS, heads, ROPE)
    lat = latent[row_of]
    kr = k_rope[row_of]
    up_key = w_uk.reshape(LAT, heads, NOPE).astype(jnp.float32)
    up_value = w_uv.reshape(LAT, heads, VDIM).astype(jnp.float32)
    lat_f = lat.astype(jnp.float32)
    kr_f = kr.astype(jnp.float32)
    group_rows = HEAD_DEV * VDIM
    block = math.gcd(TOKENS, 512)
    pieces = []
    for index in range(TOKENS // block):
        low = index * block
        high = low + block
        absorbed = jnp.einsum('thn,lhn->htl', qn[low:high].astype(jnp.float32), up_key).astype(jnp.bfloat16)
        score = jnp.einsum('htl,kl->htk', absorbed.astype(jnp.float32), lat_f[:high])
        score = score + jnp.einsum('thr,kr->htk', qr[low:high].astype(jnp.float32), kr_f[:high])
        score = score * scale
        qpos = jnp.arange(low, high, dtype=jnp.int32)
        kpos = jnp.arange(0, high, dtype=jnp.int32)
        visible = kpos[None, None, :] <= qpos[None, :, None]
        top = lax.optimization_barrier(jnp.max(jnp.where(visible, score, -1e+30), axis=-1))
        weight = jnp.where(visible, jnp.exp(score - top[..., None]), 0.0)
        total = lax.optimization_barrier(jnp.sum(weight, axis=-1))
        weight_bf = weight.astype(jnp.bfloat16)
        context = jnp.einsum('htk,kl->htl', weight_bf.astype(jnp.float32), lat_f[:high])
        context = (context / total[..., None]).astype(jnp.bfloat16)
        heads_out = jnp.einsum('htl,lhv->thv', context.astype(jnp.float32), up_value).astype(jnp.bfloat16)
        heads_out = heads_out.reshape(block, heads * VDIM)
        summed = jnp.zeros((block, D), jnp.float32)
        for group in range(N_HEAD):
            first = group * group_rows
            part = jnp.dot(heads_out[:, first:first + group_rows], w_o[first:first + group_rows], preferred_element_type=jnp.float32).astype(jnp.bfloat16)
            summed = summed + part.astype(jnp.float32)
        pieces.append(summed.astype(jnp.bfloat16))
    ordered = jnp.concatenate(pieces, axis=0)
    rows = jnp.arange(TOKENS, dtype=jnp.int32)
    place_of_row = (span_order[rows // half] * half + rows % half).astype(jnp.int32)
    return ordered[place_of_row]
```

```python
import math

import jax
import jax.numpy as jnp
from jax import lax
from jax.sharding import PartitionSpec as P

LAT = 512
ROPE = 64
NOPE = 128
VDIM = 128
AXES = ("ctx", "head")


def local(ctx_n, head_n, q_nope, q_rope, latent, k_rope, span_order, w_uk, w_uv, w_o):
    rows = q_nope.shape[0]
    half = rows // 2
    heads = w_uk.shape[1] // NOPE
    scale = 1.0 / math.sqrt(NOPE + ROPE)
    xs = head_n // 2
    zs = ctx_n // xs
    zl = zs // 2
    c = lax.axis_index("ctx")
    h = lax.axis_index("head")
    k = h % 2
    y = h // 2
    z = c // xs
    x = c % xs

    def send(value, where):
        pairs = []
        for ci in range(ctx_n):
            for hi in range(head_n):
                to = where(ci // xs, ci % xs, hi // 2, hi % 2)
                if to is not None:
                    tz, tx, ty, tk = to
                    pairs.append((ci * head_n + hi, (tz * xs + tx) * head_n + ty * 2 + tk))
        return lax.ppermute(value, AXES, pairs)

    keys = jnp.concatenate([latent, k_rope], axis=1)
    mine = lax.dynamic_slice_in_dim(keys, k * half, half, axis=0)
    spans = [mine]
    for d in range(1, ctx_n):
        dz, dx = d // xs, d % xs
        spans.append(send(mine, lambda z, x, y, k: (z ^ dz, x ^ dx, y, k)))
    got = jnp.concatenate(spans, axis=0)
    other = send(got, lambda z, x, y, k: (z, x, y, 1 - k))
    key_all = jnp.concatenate([got, other], axis=0)
    lat_piece = key_all[:, :LAT]
    rope_piece = key_all[:, LAT:]
    rel = jnp.arange(ctx_n, dtype=jnp.int32)
    slots = jnp.concatenate([2 * (c ^ rel) + k, 2 * (c ^ rel) + 1 - k])
    inside = jnp.arange(half, dtype=jnp.int32)
    kpos = (span_order[slots][:, None] * half + inside[None, :]).reshape(-1)
    qslots = 2 * c + jnp.arange(2, dtype=jnp.int32)
    qpos = (span_order[qslots][:, None] * half + inside[None, :]).reshape(-1)

    absorbed = jnp.einsum(
        "thn,lhn->htl",
        q_nope.reshape(rows, heads, NOPE),
        w_uk.reshape(LAT, heads, NOPE),
        preferred_element_type=jnp.float32,
    ).astype(jnp.bfloat16)
    rotary = q_rope.reshape(rows, heads, ROPE)
    score = jnp.einsum("htl,kl->htk", absorbed, lat_piece, preferred_element_type=jnp.float32)
    score = score + jnp.einsum(
        "thr,kr->htk", rotary, rope_piece, preferred_element_type=jnp.float32
    )
    score = score * scale
    visible = kpos[None, None, :] <= qpos[None, :, None]
    top = jnp.max(jnp.where(visible, score, -1e30), axis=-1)
    weight = jnp.where(visible, jnp.exp(score - top[..., None]), 0.0)
    total = jnp.sum(weight, axis=-1)
    accum = jnp.einsum(
        "htk,kl->htl", weight.astype(jnp.bfloat16), lat_piece, preferred_element_type=jnp.float32
    )
    context = (accum / total[..., None]).astype(jnp.bfloat16)
    heads_out = jnp.einsum(
        "htl,lhv->thv", context, w_uv.reshape(LAT, heads, VDIM), preferred_element_type=jnp.float32
    ).astype(jnp.bfloat16)
    heads_out = heads_out.reshape(rows, heads * VDIM)

    along = {0: heads_out}
    for d in range(1, zs):
        if d == 3:
            near = send(
                heads_out,
                lambda z, x, y, k: (z ^ 3, x, y, k) if abs(z - (z ^ 3)) < 3 else None,
            )
            far = send(
                along[2],
                lambda z, x, y, k: (z ^ 1, x, y, k) if abs(z - (z ^ 3)) < 3 else None,
            )
            is_near = (z % 4 == 1) | (z % 4 == 2)
            along[3] = jnp.where(is_near, near, far)
        else:
            along[d] = send(heads_out, lambda z, x, y, k: (z ^ d, x, y, k))
    blocks = [[along[d]] for d in range(zs)]
    for d in range(zs):
        for dx in range(1, xs):
            blocks[d].append(send(along[d], lambda z, x, y, k: (z, x ^ dx, y, k)))
    part = jnp.stack(
        [
            jnp.stack([jnp.dot(b, w_o, preferred_element_type=jnp.float32) for b in row])
            for row in blocks
        ]
    )
    cols = w_o.shape[1]

    two = part.reshape(2, zl, xs, rows, cols)
    keep = k ^ (z // zl)
    mine = lax.dynamic_index_in_dim(two, keep, 0, keepdims=False)
    away = lax.dynamic_index_in_dim(two, 1 - keep, 0, keepdims=False).astype(jnp.bfloat16)
    mine = mine + send(away, lambda z, x, y, k: (z, x, y, 1 - k)).astype(jnp.float32)
    bit = xs // 2
    while bit:
        two = mine.reshape(zl, 2, bit, rows, cols)
        keep = ((y ^ x) // bit) % 2
        mine = lax.dynamic_index_in_dim(two, keep, 1, keepdims=False)
        away = lax.dynamic_index_in_dim(two, 1 - keep, 1, keepdims=False).astype(jnp.bfloat16)
        step = bit
        mine = mine + send(away, lambda z, x, y, k: (z, x, y ^ step, k)).astype(jnp.float32)
        bit //= 2
    mine = mine.reshape(zl, rows, cols).astype(jnp.bfloat16)
    pieces = []
    for i in range(zl):
        out_block = lax.dynamic_index_in_dim(mine, i ^ x ^ (z % zl), 0, keepdims=False)
        pieces.append(
            send(out_block, lambda z, x, y, k: (k * zl + (i ^ x), y, z // 2, z % 2))
        )
    order = jnp.arange(zl, dtype=jnp.int32) ^ (z % zl)
    if zl == 2:
        first = jnp.where(z % 2 == 0, pieces[0], pieces[1])
        second = jnp.where(z % 2 == 0, pieces[1], pieces[0])
        return jnp.concatenate([first, second], axis=1)
    stacked = jnp.stack(pieces)[order]
    return jnp.transpose(stacked, (1, 0, 2)).reshape(rows, zl * cols)


def solution(mesh):
    placed = (
        P("ctx", "head"),
        P("ctx", "head"),
        P("ctx", None),
        P("ctx", None),
        P(),
        P(None, "head"),
        P(None, "head"),
        P("head", "ctx"),
    )
    ctx_n, head_n = mesh.shape["ctx"], mesh.shape["head"]

    def step(*args):
        return local(ctx_n, head_n, *args)

    return jax.shard_map(
        step, mesh=mesh, in_specs=placed, out_specs=P("ctx", "head"), check_vma=False
    )
```

```python
import functools
import math

import jax
import jax.numpy as jnp
from jax import lax
from jax.experimental import pallas as pl
from jax.experimental.pallas import tpu as pltpu
from jax.sharding import PartitionSpec as P

LAT = 512
ROPE = 64
NOPE = 128
VDIM = 128
AXES = ("ctx", "head")


VMEM_BYTES = 60 * 1024 * 1024


def key_kernel(latent_ref, rope_ref, out_ref):
    out_ref[:, :LAT] = latent_ref[...]
    out_ref[:, LAT:] = rope_ref[...].T


def query_kernel(heads, q_ref, rope_ref, w_ref, out_ref):
    for h in range(heads):
        cols = slice(h * NOPE, (h + 1) * NOPE)
        out_ref[h, :, :LAT] = lax.dot_general(
            q_ref[:, cols],
            w_ref[:, cols],
            (((1,), (1,)), ((), ())),
            preferred_element_type=jnp.float32,
        ).astype(jnp.bfloat16)
        out_ref[h, :, LAT:] = rope_ref[:, h * ROPE : (h + 1) * ROPE]


def attend_kernel(near, far, group, scale, span, *refs):
    order_ref, place_ref, q_ref, w_ref, own_ref = refs[:5]
    blocks = refs[5 : 5 + 2 * len(far)]
    out_ref, keys = refs[5 + 2 * len(far) :]
    heads, rows, _ = q_ref.shape
    half = rows // 2
    c = place_ref[0]
    k = place_ref[1]
    direct = blocks[: len(far)]
    passed = blocks[len(far) :]
    lane = lax.broadcasted_iota(jnp.int32, (1, rows), 1)
    places = []

    def place(distance, at, value):
        slot = 2 * (c ^ distance)
        first = order_ref[slot] * half
        second = order_ref[slot + 1] * half - half
        places.append(lane + jnp.where(lane < half, first, second))
        keys[at * rows : (at + 1) * rows, :] = value

    place(0, 0, own_ref[...])
    at = 1
    for i in range(len(far)):
        if i < len(near):
            place(jnp.where(k == 0, near[i], far[i]), at, direct[i][...])
            place(jnp.where(k == 0, far[i], near[i]), at + 1, passed[i][...])
            at += 2
        else:
            place(far[i], at, jnp.where(k == 0, passed[i][...], direct[i][...]))
            at += 1
    key_place = jnp.concatenate(places, axis=1)
    query_place = order_ref[2 * c + span] * half + lax.broadcasted_iota(jnp.int32, (half, 1), 0)
    visible = key_place <= query_place
    for g in range(heads // group):
        q = q_ref[g * group : (g + 1) * group, span * half : (span + 1) * half, :]
        score = lax.dot_general(
            q.reshape(group * half, LAT + ROPE),
            keys[...],
            (((1,), (1,)), ((), ())),
            preferred_element_type=jnp.float32,
        )
        score = score.reshape(group, half, -1) * scale
        score = jnp.where(visible[None], score, -1e30)
        top = jnp.max(score, axis=-1, keepdims=True)
        weight = jnp.exp(score - top)
        total = jnp.sum(weight, axis=-1, keepdims=True)
        accum = jnp.dot(
            weight.astype(jnp.bfloat16).reshape(group * half, -1),
            keys[:, :LAT],
            preferred_element_type=jnp.float32,
        ).reshape(group, half, LAT)
        context = (accum / total).astype(jnp.bfloat16)
        for i in range(group):
            cols = slice((g * group + i) * VDIM, (g * group + i + 1) * VDIM)
            out_ref[:, cols] = jnp.dot(
                context[i], w_ref[:, cols], preferred_element_type=jnp.float32
            ).astype(jnp.bfloat16)


def whole():
    return pl.BlockSpec(memory_space=pltpu.VMEM)


def call(kernel, shape, args, smem=0, scratch=(), flops=0, exps=0):
    moved = sum(a.size * a.dtype.itemsize for a in args)
    return pl.pallas_call(
        kernel,
        out_shape=jax.ShapeDtypeStruct(shape, jnp.bfloat16),
        in_specs=[pl.BlockSpec(memory_space=pltpu.SMEM)] * smem + [whole()] * (len(args) - smem),
        out_specs=whole(),
        scratch_shapes=list(scratch),
        compiler_params=pltpu.CompilerParams(vmem_limit_bytes=VMEM_BYTES),
        cost_estimate=pl.CostEstimate(
            flops=flops, bytes_accessed=moved + 2 * math.prod(shape), transcendentals=exps
        ),
    )(*args)


def local(ctx_n, head_n, q_nope, q_rope, latent, k_rope, span_order, w_uk, w_uv, w_o):
    rows = q_nope.shape[0]
    heads = w_uk.shape[1] // NOPE
    scale = 1.0 / math.sqrt(NOPE + ROPE)
    xs = head_n // 2
    zs = ctx_n // xs
    half = rows // 2
    c = lax.axis_index("ctx")
    h = lax.axis_index("head")
    k = h % 2
    y = h // 2
    z = c // xs
    x = c % xs

    def send(value, where):
        pairs = []
        for ci in range(ctx_n):
            for hi in range(head_n):
                to = where(ci // xs, ci % xs, hi // 2, hi % 2)
                if to is not None:
                    tz, tx, ty, tk = to
                    pairs.append((ci * head_n + hi, (tz * xs + tx) * head_n + ty * 2 + tk))
        return lax.ppermute(value, AXES, pairs)

    keys = call(key_kernel, (rows, LAT + ROPE), (latent, k_rope.T))
    split = (ctx_n - 1) // 2
    near = list(range(1, 1 + split))
    far = list(range(1 + split, ctx_n))
    direct = []
    for i in range(len(far)):
        to = (near[i] if i < split else None, far[i])

        def target(z, x, y, k):
            if to[k] is None:
                return None
            return z ^ (to[k] // xs), x ^ (to[k] % xs), y, k

        direct.append(send(keys, target))
    passed = [
        send(
            direct[i],
            lambda z, x, y, k: (z, x, y, 1 - k) if i < split or k == 1 else None,
        )
        for i in range(len(far))
    ]
    count = ctx_n * rows
    queries = call(
        functools.partial(query_kernel, heads),
        (heads, rows, LAT + ROPE),
        (q_nope, q_rope, w_uk),
        flops=2 * rows * heads * NOPE * LAT,
    )
    where_am_i = jnp.stack([c, k]).astype(jnp.int32)
    results = []
    for span in range(2):
        heads_out = call(
            functools.partial(attend_kernel, near, far, 4, scale, span),
            (half, heads * VDIM),
            (span_order, where_am_i, queries, w_uv, keys, *direct, *passed),
            smem=2,
            scratch=(pltpu.VMEM((count, LAT + ROPE), jnp.bfloat16),),
            flops=2 * half * heads * (count * (2 * LAT + ROPE) + LAT * VDIM),
            exps=half * heads * count,
        )
        results.append(project(send, zs, xs, z, x, y, k, heads_out, w_o))
    return jnp.concatenate(results, axis=0)


def project(send, zs, xs, z, x, y, k, heads_out, w_o):
    zl = zs // 2
    along = {0: heads_out}
    for d in range(1, zs):
        if d == 3:
            near = send(
                heads_out,
                lambda z, x, y, k: (z ^ 3, x, y, k) if abs(z - (z ^ 3)) < 3 else None,
            )
            far = send(
                along[2],
                lambda z, x, y, k: (z ^ 1, x, y, k) if abs(z - (z ^ 3)) < 3 else None,
            )
            is_near = (z % 4 == 1) | (z % 4 == 2)
            along[3] = jnp.where(is_near, near, far)
        else:
            along[d] = send(heads_out, lambda z, x, y, k: (z ^ d, x, y, k))
    part = {}
    for d in range(zs):
        for dx in range(xs):
            block = along[d]
            if dx:
                block = send(block, lambda z, x, y, k: (z, x ^ dx, y, k))
            part[d, dx] = jnp.dot(block, w_o, preferred_element_type=jnp.float32)

    keep = (k ^ (z // zl)) == 0
    names = [(d, dx) for d in range(zl) for dx in range(xs)]
    away = jnp.stack(
        [jnp.where(keep, part[d + zl, dx], part[d, dx]).astype(jnp.bfloat16) for d, dx in names]
    )
    got = send(away, lambda z, x, y, k: (z, x, y, 1 - k)).astype(jnp.float32)
    mine = {
        (d, dx): jnp.where(keep, part[d, dx], part[d + zl, dx]) + got[i]
        for i, (d, dx) in enumerate(names)
    }
    bit = xs // 2
    while bit:
        keep = ((y ^ x) // bit) % 2 == 0
        names = [(d, dx) for d in range(zl) for dx in range(bit)]
        away = jnp.stack(
            [
                jnp.where(keep, mine[d, dx + bit], mine[d, dx]).astype(jnp.bfloat16)
                for d, dx in names
            ]
        )
        step = bit
        got = send(away, lambda z, x, y, k: (z, x, y ^ step, k)).astype(jnp.float32)
        mine = {
            (d, dx): jnp.where(keep, mine[d, dx], mine[d, dx + bit]) + got[i]
            for i, (d, dx) in enumerate(names)
        }
        bit //= 2
    mine = [mine[d, 0].astype(jnp.bfloat16) for d in range(zl)]
    at = x ^ (z % zl)
    pieces = [
        send(
            choose(mine, i ^ at),
            lambda z, x, y, k: (k * zl + (i ^ x), y, z // 2, z % 2),
        )
        for i in range(zl)
    ]
    return jnp.concatenate([choose(pieces, i ^ (z % zl)) for i in range(zl)], axis=1)


def choose(values, index):
    out = values[0]
    for i in range(1, len(values)):
        out = jnp.where(index == i, values[i], out)
    return out


def solution(mesh):
    placed = (
        P("ctx", "head"),
        P("ctx", "head"),
        P("ctx", None),
        P("ctx", None),
        P(),
        P(None, "head"),
        P(None, "head"),
        P("head", "ctx"),
    )
    ctx_n, head_n = mesh.shape["ctx"], mesh.shape["head"]

    def step(*args):
        return local(ctx_n, head_n, *args)

    return jax.shard_map(
        step, mesh=mesh, in_specs=placed, out_specs=P("ctx", "head"), check_vma=False
    )
```

```python
import functools
import math

import jax
import jax.numpy as jnp
from jax import lax
from jax.experimental import pallas as pl
from jax.experimental.pallas import tpu as pltpu
from jax.sharding import PartitionSpec as P

LAT = 512
ROPE = 64
NOPE = 128
VDIM = 128
AXES = ("ctx", "head")
MIB = 1024 * 1024
NT = (((1,), (1,)), ((), ()))


def key_kernel(latent_ref, rope_ref, out_ref):
    out_ref[:, :LAT] = latent_ref[...]
    out_ref[:, LAT:] = rope_ref[...].T


def query_kernel(q_ref, rope_ref, w_ref, out_ref):
    for h in range(out_ref.shape[0]):
        cols = slice(h * NOPE, (h + 1) * NOPE)
        out_ref[h, :, :LAT] = lax.dot_general(
            q_ref[:, cols], w_ref[:, cols], NT, preferred_element_type=jnp.float32
        ).astype(jnp.bfloat16)
        out_ref[h, :, LAT:] = rope_ref[:, h * ROPE : (h + 1) * ROPE]


def place_keys(pairs, order_ref, place_ref, own_ref, direct, passed, keys):
    rows = direct[0].shape[0]
    half = rows // 2
    c = place_ref[0]
    k = place_ref[1]
    lane = lax.broadcasted_iota(jnp.int32, (1, rows), 1)
    places = []

    def add(distance, value):
        slot = 2 * (c ^ distance)
        first = order_ref[slot] * half
        second = order_ref[slot + 1] * half - half
        at = len(places) * rows
        keys[at : at + rows, :] = value
        places.append(lane + jnp.where(lane < half, first, second))

    if own_ref is not None:
        add(0, own_ref[...])
    for (on_0, on_1), mine, other in zip(pairs, direct, passed):
        if on_0 is None:
            add(on_1, jnp.where(k == 0, other[...], mine[...]))
        else:
            add(jnp.where(k == 0, on_0, on_1), mine[...])
            add(jnp.where(k == 0, on_1, on_0), other[...])
    return jnp.concatenate(places, axis=1)


def early_kernel(pairs, group, scale, order_ref, place_ref, q_ref, own_ref, *refs):
    n = len(pairs)
    out_ref, keys = refs[2 * n :]
    key_place = place_keys(
        pairs, order_ref, place_ref, own_ref, refs[:n], refs[n : 2 * n], keys
    )
    heads, rows, _ = q_ref.shape
    half = rows // 2
    c = place_ref[0]
    row = lax.broadcasted_iota(jnp.int32, (rows, 1), 0)
    first = order_ref[2 * c] * half
    second = order_ref[2 * c + 1] * half - half
    visible = key_place <= row + jnp.where(row < half, first, second)
    lane = lax.broadcasted_iota(jnp.int32, (1, 1, 128), 2)
    for g in range(0, heads, group):
        q = q_ref[g : g + group].reshape(group * rows, LAT + ROPE)
        score = lax.dot_general(q, keys[...], NT, preferred_element_type=jnp.float32)
        score = score.reshape(group, rows, -1) * scale
        score = jnp.where(visible[None], score, -1e30)
        top = jnp.max(score, axis=-1, keepdims=True)
        weight = jnp.exp(score - top)
        total = jnp.sum(weight, axis=-1, keepdims=True)
        weight = weight.astype(jnp.bfloat16).reshape(group * rows, -1)
        accum = jnp.dot(weight, keys[:, :LAT], preferred_element_type=jnp.float32)
        out_ref[g : g + group, :, :LAT] = accum.reshape(group, rows, LAT)
        out_ref[g : g + group, :, LAT:] = jnp.where(lane == 0, top, total)


def late_kernel(pairs, group, scale, span, order_ref, place_ref, q_ref, w_ref, early_ref, *refs):
    n = len(pairs)
    out_ref, keys = refs[2 * n :]
    key_place = place_keys(pairs, order_ref, place_ref, None, refs[:n], refs[n : 2 * n], keys)
    heads, rows, _ = q_ref.shape
    half = rows // 2
    c = place_ref[0]
    row = lax.broadcasted_iota(jnp.int32, (half, 1), 0)
    visible = key_place <= row + order_ref[2 * c + span] * half
    these = slice(span * half, (span + 1) * half)
    for g in range(0, heads, group):
        q = q_ref[g : g + group, these, :].reshape(group * half, LAT + ROPE)
        score = lax.dot_general(q, keys[...], NT, preferred_element_type=jnp.float32)
        score = score.reshape(group, half, -1) * scale
        score = jnp.where(visible[None], score, -1e30)
        old = early_ref[g : g + group, these, LAT : LAT + 1]
        total = early_ref[g : g + group, these, LAT + 1 : LAT + 2]
        top = jnp.maximum(old, jnp.max(score, axis=-1, keepdims=True))
        fade = jnp.exp(old - top)
        weight = jnp.exp(score - top)
        total = total * fade + jnp.sum(weight, axis=-1, keepdims=True)
        weight = weight.astype(jnp.bfloat16).reshape(group * half, -1)
        accum = jnp.dot(weight, keys[:, :LAT], preferred_element_type=jnp.float32)
        accum = accum.reshape(group, half, LAT) + early_ref[g : g + group, these, :LAT] * fade
        context = (accum / total).astype(jnp.bfloat16)
        for i in range(group):
            cols = slice((g + i) * VDIM, (g + i + 1) * VDIM)
            out_ref[:, cols] = jnp.dot(
                context[i], w_ref[:, cols], preferred_element_type=jnp.float32
            ).astype(jnp.bfloat16)


def project_kernel(zs, xs, kept, place_ref, *refs):
    blocks, weights, out_ref = refs[: zs + 2], refs[zs + 2 : -1], refs[-1]
    zl = zs // 2
    k = place_ref[1]
    z = place_ref[2]
    x = place_ref[3]
    inner = (z % 4 == 1) | (z % 4 == 2)
    low_half = (k ^ (z // zl)) == 0 if kept else (k ^ (z // zl)) == 1

    def block(d):
        if d < 2:
            return blocks[d][...]
        if d < 4:
            at = 2 * d - 2
            return jnp.where(inner, blocks[at][...], blocks[at + 1][...])
        return blocks[d + 2][...]

    rows = blocks[0].shape[0]
    tokens = jnp.concatenate(
        [jnp.where(low_half, block(d), block(d + zl)) for d in range(zl)], axis=0
    )
    for dx in range(xs):
        part = jnp.dot(tokens, weights[dx][...], preferred_element_type=jnp.float32)
        part = part.astype(out_ref.dtype).reshape(zl, rows, -1)
        for d in range(zl):
            out_ref[d, x ^ dx] = part[d]


def halve_kernel(bit, span, place_ref, mine_ref, got_ref, keep_ref, away_ref):
    which = place_ref[4 + span]
    low = ((which // bit) % 2) == 0
    for d in range(bit):
        a = mine_ref[d] + got_ref[d].astype(jnp.float32)
        b = mine_ref[d + bit] + got_ref[d + bit].astype(jnp.float32)
        keep_ref[d] = jnp.where(low, a, b)
        away_ref[d] = jnp.where(low, b, a).astype(away_ref.dtype)


def add_kernel(mine_ref, got_ref, out_ref):
    out_ref[...] = (mine_ref[0] + got_ref[0].astype(jnp.float32)).astype(out_ref.dtype)


def output_kernel(*refs):
    out_ref = refs[-1]
    for span, ref in enumerate(refs[:-1]):
        xs, half, cols = ref.shape
        for i in range(xs):
            out_ref[span * half : (span + 1) * half, i * cols : (i + 1) * cols] = ref[i]


def whole():
    return pl.BlockSpec(memory_space=pltpu.VMEM)


def call(kernel, outs, args, smem=0, scratch=(), vmem=16, flops=0, exps=0):
    several = isinstance(outs, list)
    outs = outs if several else [outs]
    shapes = [jax.ShapeDtypeStruct(shape, kind) for shape, kind in outs]
    moved = sum(a.size * a.dtype.itemsize for a in [*args, *shapes])
    result = pl.pallas_call(
        kernel,
        out_shape=shapes,
        in_specs=[pl.BlockSpec(memory_space=pltpu.SMEM)] * smem + [whole()] * (len(args) - smem),
        out_specs=[whole()] * len(shapes),
        scratch_shapes=list(scratch),
        compiler_params=pltpu.CompilerParams(vmem_limit_bytes=vmem * MIB),
        cost_estimate=pl.CostEstimate(flops=flops, bytes_accessed=moved, transcendentals=exps),
    )(*args)
    return result if several else result[0]


def local(ctx_n, head_n, q_nope, q_rope, latent, k_rope, span_order, w_uk, w_uv, w_o):
    rows = q_nope.shape[0]
    half = rows // 2
    heads = w_uk.shape[1] // NOPE
    depth, cols = w_o.shape
    scale = 1.0 / math.sqrt(NOPE + ROPE)
    xs = head_n // 2
    zs = ctx_n // xs
    zl = zs // 2
    c = lax.axis_index("ctx")
    h = lax.axis_index("head")
    k, y, z, x = h % 2, h // 2, c // xs, c % xs
    place = jnp.stack([c, k, z, x, y ^ (z % zl), y ^ (z % zl) ^ (zl - 1)]).astype(jnp.int32)
    bf16, f32 = jnp.bfloat16, jnp.float32

    def send(value, where):
        pairs = []
        for ci in range(ctx_n):
            for hi in range(head_n):
                to = where(ci // xs, ci % xs, hi // 2, hi % 2)
                if to is not None:
                    tz, tx, ty, tk = to
                    pairs.append((ci * head_n + hi, (tz * xs + tx) * head_n + ty * 2 + tk))
        return lax.ppermute(value, AXES, pairs)

    keys = call(key_kernel, ((rows, LAT + ROPE), bf16), (latent, k_rope.T), vmem=4)
    pairs = [(d, d + 1) for d in range(1, ctx_n - 1, 2)] + [(None, ctx_n - 1)]

    def across(pair):
        def where(z, x, y, k):
            d = pair[k]
            return None if d is None else (z ^ (d // xs), x ^ (d % xs), y, k)

        return where

    def to_other(pair):
        return lambda z, x, y, k: (z, x, y, 1 - k) if pair[k] is not None else None

    def inner_only(where):
        return lambda z, x, y, k: where(z, x, y, k) if z % 4 in (1, 2) else None

    direct = []
    for pair in pairs:
        direct.append(send(keys, across(pair)))
    matrices = [w_o] + [
        send(w_o, lambda z, x, y, k: (z, x ^ dx, y, k)) for dx in range(1, xs)
    ]
    queries = call(
        query_kernel,
        ((heads, rows, LAT + ROPE), bf16),
        (q_nope, q_rope, w_uk),
        flops=2 * rows * heads * NOPE * LAT,
    )
    first = len(pairs) // 2
    direct[:first], queries = lax.optimization_barrier((direct[:first], queries))
    passed = [send(direct[i], to_other(pairs[i])) for i in range(first)]
    n_early = 1 + 2 * first
    n_late = ctx_n - n_early

    def work(queries_n, keys_n):
        return 2 * queries_n * heads * keys_n * (2 * LAT + ROPE)

    early = call(
        functools.partial(early_kernel, pairs[:first], 2, scale),
        ((heads, rows, LAT + 128), f32),
        (span_order, place, queries, keys, *direct[:first], *passed[:first]),
        smem=2,
        scratch=(pltpu.VMEM((n_early * rows, LAT + ROPE), bf16),),
        vmem=32,
        flops=work(rows, n_early * rows),
        exps=rows * heads * n_early * rows,
    )
    direct[first:], early = lax.optimization_barrier((direct[first:], early))
    passed += [send(direct[i], to_other(pairs[i])) for i in range(first, len(pairs))]
    results = []
    for span in range(2):
        flip = span * (zl - 1)
        heads_out = call(
            functools.partial(late_kernel, pairs[first:], 4, scale, span),
            ((half, heads * VDIM), bf16),
            (span_order, place, queries, w_uv, early, *direct[first:], *passed[first:]),
            smem=2,
            scratch=(pltpu.VMEM((n_late * rows, LAT + ROPE), bf16),),
            vmem=32,
            flops=work(half, n_late * rows) + 2 * half * heads * LAT * VDIM,
            exps=half * heads * n_late * rows,
        )
        beside = send(heads_out, lambda z, x, y, k: (z ^ 1, x, y, k))
        middle = send(heads_out, inner_only(lambda z, x, y, k: (z ^ 3, x, y, k)))
        outer_2 = send(middle, inner_only(lambda z, x, y, k: (z ^ 1, x, y, k)))
        inner_2 = send(beside, inner_only(lambda z, x, y, k: (z ^ 3, x, y, k)))
        outer_3 = send(inner_2, inner_only(lambda z, x, y, k: (z ^ 1, x, y, k)))
        along = [heads_out, beside, inner_2, outer_2, middle, outer_3]
        along += [
            send(heads_out, lambda z, x, y, k: (z ^ d, x, y, k)) for d in range(4, zs)
        ]

        def project(kept, kind):
            return call(
                functools.partial(project_kernel, zs, xs, kept),
                ((zl, xs, half, cols), kind),
                (place, *along, *matrices),
                smem=1,
                flops=2 * zl * half * depth * xs * cols,
            )

        away = project(False, bf16)
        got = send(away, lambda z, x, y, k: (z, x, y, 1 - k))
        mine = project(True, f32)
        bit = zl // 2
        while bit:
            block = (bit, xs, half, cols)
            mine, away = call(
                functools.partial(halve_kernel, bit, span),
                [(block, f32), (block, bf16)],
                (place, mine, got),
                smem=1,
            )
            got = send(away, lambda z, x, y, k: (z, x, y ^ bit, k))
            bit //= 2
        block = call(add_kernel, ((xs, half, cols), bf16), (mine, got))
        results.append(send(block, lambda z, x, y, k: (k * zl + (y ^ flip), x, z // 2, z % 2)))
    return call(output_kernel, ((rows, xs * cols), bf16), tuple(results))


def solution(mesh):
    placed = (
        P("ctx", "head"),
        P("ctx", "head"),
        P("ctx", None),
        P("ctx", None),
        P(),
        P(None, "head"),
        P(None, "head"),
        P("head", "ctx"),
    )
    ctx_n, head_n = mesh.shape["ctx"], mesh.shape["head"]

    def step(*args):
        return local(ctx_n, head_n, *args)

    return jax.shard_map(
        step, mesh=mesh, in_specs=placed, out_specs=P("ctx", "head"), check_vma=False
    )
```

```python
import functools
import math

import jax
import jax.numpy as jnp
from jax import lax
from jax.experimental import pallas as pl
from jax.experimental.pallas import tpu as pltpu
from jax.sharding import PartitionSpec as P

LAT = 512
ROPE = 64
NOPE = 128
VDIM = 128
AXES = ("ctx", "head")
MIB = 1024 * 1024
NT = (((1,), (1,)), ((), ()))


def key_kernel(latent_ref, rope_ref, out_ref):
    out_ref[:, :LAT] = latent_ref[...]
    out_ref[:, LAT:] = rope_ref[...].T


def query_kernel(q_ref, rope_ref, w_ref, out_ref):
    for h in range(out_ref.shape[0]):
        cols = slice(h * NOPE, (h + 1) * NOPE)
        out_ref[h, :, :LAT] = lax.dot_general(
            q_ref[:, cols], w_ref[:, cols], NT, preferred_element_type=jnp.float32
        ).astype(jnp.bfloat16)
        out_ref[h, :, LAT:] = rope_ref[:, h * ROPE : (h + 1) * ROPE]


def place_keys(pairs, order_ref, place_ref, own_ref, direct, passed, keys):
    rows = direct[0].shape[0]
    half = rows // 2
    c = place_ref[0]
    k = place_ref[1]
    lane = lax.broadcasted_iota(jnp.int32, (1, rows), 1)
    places = []

    def add(distance, value):
        slot = 2 * (c ^ distance)
        first = order_ref[slot] * half
        second = order_ref[slot + 1] * half - half
        at = len(places) * rows
        keys[at : at + rows, :] = value
        places.append(lane + jnp.where(lane < half, first, second))

    if own_ref is not None:
        add(0, own_ref[...])
    for (on_0, on_1), mine, other in zip(pairs, direct, passed):
        if on_0 is None:
            add(on_1, jnp.where(k == 0, other[...], mine[...]))
        else:
            add(jnp.where(k == 0, on_0, on_1), mine[...])
            add(jnp.where(k == 0, on_1, on_0), other[...])
    return jnp.concatenate(places, axis=1)


def early_kernel(pairs, group, scale, order_ref, place_ref, q_ref, own_ref, *refs):
    n = len(pairs)
    out_ref, keys = refs[2 * n :]
    key_place = place_keys(
        pairs, order_ref, place_ref, own_ref, refs[:n], refs[n : 2 * n], keys
    )
    heads, rows, _ = q_ref.shape
    half = rows // 2
    c = place_ref[0]
    row = lax.broadcasted_iota(jnp.int32, (rows, 1), 0)
    first = order_ref[2 * c] * half
    second = order_ref[2 * c + 1] * half - half
    visible = key_place <= row + jnp.where(row < half, first, second)
    lane = lax.broadcasted_iota(jnp.int32, (1, 1, 128), 2)
    for g in range(0, heads, group):
        q = q_ref[g : g + group].reshape(group * rows, LAT + ROPE)
        score = lax.dot_general(q, keys[...], NT, preferred_element_type=jnp.float32)
        score = score.reshape(group, rows, -1) * scale
        score = jnp.where(visible[None], score, -1e30)
        top = jnp.max(score, axis=-1, keepdims=True)
        weight = jnp.exp(score - top)
        total = jnp.sum(weight, axis=-1, keepdims=True)
        weight = weight.astype(jnp.bfloat16).reshape(group * rows, -1)
        accum = jnp.dot(weight, keys[:, :LAT], preferred_element_type=jnp.float32)
        out_ref[g : g + group, :, :LAT] = accum.reshape(group, rows, LAT)
        out_ref[g : g + group, :, LAT:] = jnp.where(lane == 0, top, total)


def late_kernel(pairs, group, scale, span, order_ref, place_ref, q_ref, w_ref, early_ref, *refs):
    n = len(pairs)
    out_ref, keys = refs[2 * n :]
    key_place = place_keys(pairs, order_ref, place_ref, None, refs[:n], refs[n : 2 * n], keys)
    heads, rows, _ = q_ref.shape
    half = rows // 2
    c = place_ref[0]
    row = lax.broadcasted_iota(jnp.int32, (half, 1), 0)
    visible = key_place <= row + order_ref[2 * c + span] * half
    these = slice(span * half, (span + 1) * half)
    for g in range(0, heads, group):
        q = q_ref[g : g + group, these, :].reshape(group * half, LAT + ROPE)
        score = lax.dot_general(q, keys[...], NT, preferred_element_type=jnp.float32)
        score = score.reshape(group, half, -1) * scale
        score = jnp.where(visible[None], score, -1e30)
        old = early_ref[g : g + group, these, LAT : LAT + 1]
        total = early_ref[g : g + group, these, LAT + 1 : LAT + 2]
        top = jnp.maximum(old, jnp.max(score, axis=-1, keepdims=True))
        fade = jnp.exp(old - top)
        weight = jnp.exp(score - top)
        total = total * fade + jnp.sum(weight, axis=-1, keepdims=True)
        weight = weight.astype(jnp.bfloat16).reshape(group * half, -1)
        accum = jnp.dot(weight, keys[:, :LAT], preferred_element_type=jnp.float32)
        accum = accum.reshape(group, half, LAT) + early_ref[g : g + group, these, :LAT] * fade
        context = (accum / total).astype(jnp.bfloat16)
        for i in range(group):
            cols = slice((g + i) * VDIM, (g + i + 1) * VDIM)
            out_ref[:, cols] = jnp.dot(
                context[i], w_ref[:, cols], preferred_element_type=jnp.float32
            ).astype(jnp.bfloat16)


def ring_place(z, zs):
    return jnp.where(z % 2 == 1, (z + 1) // 2, (zs - z // 2) % zs)


def ring_member(at, zs):
    return jnp.where(at > zs // 2, 2 * (zs - at), jnp.maximum(2 * at - 1, 0))


def project_kernel(zs, kept, place_ref, w_ref, *refs):
    blocks, out_ref, tokens = refs[:-2], refs[-2], refs[-1]
    zl = zs // 2
    k = place_ref[1]
    half = blocks[0].shape[0]
    rows = half * len(blocks) // zs
    for i, block in enumerate(blocks):
        span, step = divmod(i, zs)
        member = ring_member((ring_place(place_ref[2], zs) + zs - step) % zs, zs)
        tokens[pl.ds(pl.multiple_of(member * rows + span * half, half), half), :] = block[...]
    side = k if kept else 1 - k
    these = tokens[pl.ds(pl.multiple_of(side * (zl * rows), zl * rows), zl * rows), :]
    part = jnp.dot(these, w_ref[...], preferred_element_type=jnp.float32)
    out_ref[...] = part.astype(out_ref.dtype).reshape(out_ref.shape)


def halve_kernel(bit, turn, place_ref, mine_ref, *refs):
    got_refs, keep_ref, away_refs = refs[:-3], refs[-3], refs[-2:]
    half = away_refs[0].shape[1]
    for span, away_ref in enumerate(away_refs):
        these = slice(span * half, (span + 1) * half)
        low = ((place_ref[4 + (turn + span) % 2] // bit) % 2) == 0

        def total(d):
            if len(got_refs) == 1:
                got = got_refs[0][d, these]
            else:
                got = got_refs[span][d]
            return mine_ref[d, these] + got.astype(jnp.float32)

        for d in range(bit):
            a = total(d)
            b = total(d + bit)
            keep_ref[d, these] = jnp.where(low, a, b)
            away_ref[d] = jnp.where(low, b, a).astype(away_ref.dtype)


def add_kernel(span, mine_ref, got_ref, out_ref):
    half = out_ref.shape[0]
    mine = mine_ref[0, span * half : (span + 1) * half]
    out_ref[...] = (mine + got_ref[0].astype(jnp.float32)).astype(out_ref.dtype)


def output_kernel(place_ref, *refs):
    blocks, out_ref = refs[:-1], refs[-1]
    xs = len(blocks) // 2
    x = place_ref[3]
    half, cols = blocks[0].shape
    for i in range(xs):
        for span in range(2):
            block = blocks[span][...]
            for dx in range(1, xs):
                block = jnp.where((x ^ i) == dx, blocks[2 * dx + span][...], block)
            out_ref[span * half : (span + 1) * half, i * cols : (i + 1) * cols] = block


def whole():
    return pl.BlockSpec(memory_space=pltpu.VMEM)


def call(kernel, outs, args, smem=0, scratch=(), vmem=16, flops=0, exps=0):
    several = isinstance(outs, list)
    outs = outs if several else [outs]
    shapes = [jax.ShapeDtypeStruct(shape, kind) for shape, kind in outs]
    moved = sum(a.size * a.dtype.itemsize for a in [*args, *shapes])
    result = pl.pallas_call(
        kernel,
        out_shape=shapes,
        in_specs=[pl.BlockSpec(memory_space=pltpu.SMEM)] * smem + [whole()] * (len(args) - smem),
        out_specs=[whole()] * len(shapes),
        scratch_shapes=list(scratch),
        compiler_params=pltpu.CompilerParams(vmem_limit_bytes=vmem * MIB),
        cost_estimate=pl.CostEstimate(flops=flops, bytes_accessed=moved, transcendentals=exps),
    )(*args)
    return result if several else result[0]


def local(ctx_n, head_n, q_nope, q_rope, latent, k_rope, span_order, w_uk, w_uv, w_o):
    rows = q_nope.shape[0]
    half = rows // 2
    heads = w_uk.shape[1] // NOPE
    depth, cols = w_o.shape
    scale = 1.0 / math.sqrt(NOPE + ROPE)
    xs = head_n // 2
    zs = ctx_n // xs
    zl = zs // 2
    c = lax.axis_index("ctx")
    h = lax.axis_index("head")
    k, y, z, x = h % 2, h // 2, c // xs, c % xs
    place = jnp.stack([c, k, z, x, y, y ^ (zl - 1)]).astype(jnp.int32)
    bf16, f32 = jnp.bfloat16, jnp.float32

    def send(value, where):
        pairs = []
        for ci in range(ctx_n):
            for hi in range(head_n):
                to = where(ci // xs, ci % xs, hi // 2, hi % 2)
                if to is not None:
                    tz, tx, ty, tk = to
                    pairs.append((ci * head_n + hi, (tz * xs + tx) * head_n + ty * 2 + tk))
        return lax.ppermute(value, AXES, pairs)

    keys = call(key_kernel, ((rows, LAT + ROPE), bf16), (latent, k_rope.T), vmem=60)
    pairs = [(d, d + 1) for d in range(1, ctx_n - 1, 2)] + [(None, ctx_n - 1)]

    def across(pair):
        def where(z, x, y, k):
            d = pair[k]
            return None if d is None else (z ^ (d // xs), x ^ (d % xs), y, k)

        return where

    def to_other(pair):
        return lambda z, x, y, k: (z, x, y, 1 - k) if pair[k] is not None else None

    ring = [0, *range(1, zs, 2), *range(zs - 2, 0, -2)]
    following = {z: ring[(i + 1) % zs] for i, z in enumerate(ring)}

    direct = []
    for pair in pairs:
        direct.append(send(keys, across(pair)))
    matrices = [w_o] + [
        send(w_o, lambda z, x, y, k: (z, x ^ dx, y, k)) for dx in range(1, xs)
    ]
    queries = call(
        query_kernel,
        ((heads, rows, LAT + ROPE), bf16),
        (q_nope, q_rope, w_uk),
        vmem=60,
        flops=2 * rows * heads * NOPE * LAT,
    )
    first = len(pairs) // 2
    direct[:first], queries = lax.optimization_barrier((direct[:first], queries))
    passed = [send(direct[i], to_other(pairs[i])) for i in range(first)]
    n_early = 1 + 2 * first
    n_late = ctx_n - n_early

    def work(queries_n, keys_n):
        return 2 * queries_n * heads * keys_n * (2 * LAT + ROPE)

    early = call(
        functools.partial(early_kernel, pairs[:first], 2, scale),
        ((heads, rows, LAT + 128), f32),
        (span_order, place, queries, keys, *direct[:first], *passed[:first]),
        smem=2,
        scratch=(pltpu.VMEM((n_early * rows, LAT + ROPE), bf16),),
        vmem=32,
        flops=work(rows, n_early * rows),
        exps=rows * heads * n_early * rows,
    )
    direct[first:], early = lax.optimization_barrier((direct[first:], early))
    passed += [send(direct[i], to_other(pairs[i])) for i in range(first, len(pairs))]
    blocks = []
    for span in range(2):
        heads_out = call(
            functools.partial(late_kernel, pairs[first:], 4, scale, span),
            ((half, heads * VDIM), bf16),
            (span_order, place, queries, w_uv, early, *direct[first:], *passed[first:]),
            smem=2,
            scratch=(pltpu.VMEM((n_late * rows, LAT + ROPE), bf16),),
            vmem=32,
            flops=work(half, n_late * rows) + 2 * half * heads * LAT * VDIM,
            exps=half * heads * n_late * rows,
        )
        along = [heads_out]
        for _ in range(1, zs):
            along.append(send(along[-1], lambda z, x, y, k: (following[z], x, y, k)))
        blocks += along

    results = []
    for dx in range(xs):
        turn = dx % 2
        if dx:
            matrices[dx], mine = lax.optimization_barrier((matrices[dx], mine))

        def project(kept, kind):
            return call(
                functools.partial(project_kernel, zs, kept),
                ((zl, rows, cols), kind),
                (place, matrices[dx], *blocks),
                smem=1,
                scratch=(pltpu.VMEM((zs * rows, depth), bf16),),
                flops=2 * zl * rows * depth * cols,
            )

        away = project(False, bf16)
        got = [send(away, lambda z, x, y, k: (z, x, y, 1 - k))]
        mine = project(True, f32)
        bit = zl // 2
        while bit:
            part = ((bit, half, cols), bf16)
            mine, *away = call(
                functools.partial(halve_kernel, bit, turn),
                [((bit, rows, cols), f32), part, part],
                (place, mine, *got),
                smem=1,
            )
            got = [send(value, lambda z, x, y, k: (z, x, y ^ bit, k)) for value in away]
            bit //= 2
        for span in range(2):
            block = call(
                functools.partial(add_kernel, span), ((half, cols), bf16), (mine, got[span])
            )
            flip = (turn + span) % 2 * (zl - 1)
            results.append(
                send(block, lambda z, x, y, k: (k * zl + (y ^ flip), x, z // 2, z % 2))
            )
    return call(output_kernel, ((rows, xs * cols), bf16), (place, *results), smem=1)


def solution(mesh):
    placed = (
        P("ctx", "head"),
        P("ctx", "head"),
        P("ctx", None),
        P("ctx", None),
        P(),
        P(None, "head"),
        P(None, "head"),
        P("head", "ctx"),
    )
    ctx_n, head_n = mesh.shape["ctx"], mesh.shape["head"]

    def step(*args):
        return local(ctx_n, head_n, *args)

    return jax.shard_map(
        step, mesh=mesh, in_specs=placed, out_specs=P("ctx", "head"), check_vma=False
    )
```

```python
import functools
import math

import jax
import jax.numpy as jnp
from jax import lax
from jax.experimental import pallas as pl
from jax.experimental.pallas import tpu as pltpu
from jax.sharding import PartitionSpec as P

LAT = 512
ROPE = 64
NOPE = 128
VDIM = 128
AXES = ("ctx", "head")
MIB = 1024 * 1024
COUNTS = ([1], [1])
NT = (((1,), (1,)), ((), ()))


def key_kernel(latent_ref, rope_ref, out_ref):
    out_ref[:, :LAT] = latent_ref[...]
    out_ref[:, LAT:] = rope_ref[...].T


def query_kernel(q_ref, rope_ref, w_ref, out_ref):
    for h in range(out_ref.shape[0]):
        cols = slice(h * NOPE, (h + 1) * NOPE)
        out_ref[h, :, :LAT] = lax.dot_general(
            q_ref[:, cols], w_ref[:, cols], NT, preferred_element_type=jnp.float32
        ).astype(jnp.bfloat16)
        out_ref[h, :, LAT:] = rope_ref[:, h * ROPE : (h + 1) * ROPE]


def place_keys(pairs, order_ref, place_ref, own_ref, direct, passed, keys):
    rows = direct[0].shape[0]
    half = rows // 2
    c = place_ref[0]
    k = place_ref[1]
    lane = lax.broadcasted_iota(jnp.int32, (1, rows), 1)
    places = []

    def add(distance, value):
        slot = 2 * (c ^ distance)
        first = order_ref[slot] * half
        second = order_ref[slot + 1] * half - half
        at = len(places) * rows
        keys[at : at + rows, :] = value
        places.append(lane + jnp.where(lane < half, first, second))

    if own_ref is not None:
        add(0, own_ref[...])
    for (on_0, on_1), mine, other in zip(pairs, direct, passed):
        if on_0 is None:
            add(on_1, jnp.where(k == 0, other[...], mine[...]))
        else:
            add(jnp.where(k == 0, on_0, on_1), mine[...])
            add(jnp.where(k == 0, on_1, on_0), other[...])
    return jnp.concatenate(places, axis=1)


def early_kernel(pairs, group, scale, order_ref, place_ref, q_ref, own_ref, *refs):
    n = len(pairs)
    out_ref, keys = refs[2 * n :]
    key_place = place_keys(
        pairs, order_ref, place_ref, own_ref, refs[:n], refs[n : 2 * n], keys
    )
    heads, rows, _ = q_ref.shape
    half = rows // 2
    c = place_ref[0]
    row = lax.broadcasted_iota(jnp.int32, (rows, 1), 0)
    first = order_ref[2 * c] * half
    second = order_ref[2 * c + 1] * half - half
    visible = key_place <= row + jnp.where(row < half, first, second)
    lane = lax.broadcasted_iota(jnp.int32, (1, 1, 128), 2)
    for g in range(0, heads, group):
        q = q_ref[g : g + group].reshape(group * rows, LAT + ROPE)
        score = lax.dot_general(q, keys[...], NT, preferred_element_type=jnp.float32)
        score = score.reshape(group, rows, -1) * scale
        score = jnp.where(visible[None], score, -1e30)
        top = jnp.max(score, axis=-1, keepdims=True)
        weight = jnp.exp(score - top)
        total = jnp.sum(weight, axis=-1, keepdims=True)
        weight = weight.astype(jnp.bfloat16).reshape(group * rows, -1)
        accum = jnp.dot(weight, keys[:, :LAT], preferred_element_type=jnp.float32)
        out_ref[g : g + group, :, :LAT] = accum.reshape(group, rows, LAT)
        out_ref[g : g + group, :, LAT:] = jnp.where(lane == 0, top, total)


def late_kernel(pairs, group, scale, span, order_ref, place_ref, q_ref, w_ref, early_ref, *refs):
    n = len(pairs)
    out_ref, keys = refs[2 * n :]
    key_place = place_keys(pairs, order_ref, place_ref, None, refs[:n], refs[n : 2 * n], keys)
    heads, rows, _ = q_ref.shape
    half = rows // 2
    c = place_ref[0]
    row = lax.broadcasted_iota(jnp.int32, (half, 1), 0)
    visible = key_place <= row + order_ref[2 * c + span] * half
    these = slice(span * half, (span + 1) * half)
    for g in range(0, heads, group):
        q = q_ref[g : g + group, these, :].reshape(group * half, LAT + ROPE)
        score = lax.dot_general(q, keys[...], NT, preferred_element_type=jnp.float32)
        score = score.reshape(group, half, -1) * scale
        score = jnp.where(visible[None], score, -1e30)
        old = early_ref[g : g + group, these, LAT : LAT + 1]
        total = early_ref[g : g + group, these, LAT + 1 : LAT + 2]
        top = jnp.maximum(old, jnp.max(score, axis=-1, keepdims=True))
        fade = jnp.exp(old - top)
        weight = jnp.exp(score - top)
        total = total * fade + jnp.sum(weight, axis=-1, keepdims=True)
        weight = weight.astype(jnp.bfloat16).reshape(group * half, -1)
        accum = jnp.dot(weight, keys[:, :LAT], preferred_element_type=jnp.float32)
        accum = accum.reshape(group, half, LAT) + early_ref[g : g + group, these, :LAT] * fade
        context = (accum / total).astype(jnp.bfloat16)
        for i in range(group):
            cols = slice((g + i) * VDIM, (g + i + 1) * VDIM)
            out_ref[:, cols] = jnp.dot(
                context[i], w_ref[:, cols], preferred_element_type=jnp.float32
            ).astype(jnp.bfloat16)


def ring_place(z, zs):
    return jnp.where(z % 2 == 1, (z + 1) // 2, (zs - z // 2) % zs)


def ring_member(at, zs):
    return jnp.where(at > zs // 2, 2 * (zs - at), jnp.maximum(2 * at - 1, 0))


def project_kernel(zs, place_ref, w_ref, *refs):
    blocks, mine_ref, away_ref, tokens = refs[:zs], refs[zs], refs[zs + 1], refs[zs + 2]
    zl = zs // 2
    k = place_ref[1]
    half = blocks[0].shape[0]
    for step, block in enumerate(blocks):
        member = ring_member((ring_place(place_ref[2], zs) + zs - step) % zs, zs)
        at = jnp.where(member // zl == k, 0, zl) + member % zl
        tokens[pl.ds(pl.multiple_of(at * half, half), half), :] = block[...]
    part = jnp.dot(tokens[...], w_ref[...], preferred_element_type=jnp.float32)
    part = part.reshape(zs, half, -1)
    mine_ref[...] = part[:zl]
    away_ref[...] = part[zl:].astype(away_ref.dtype)


def halve_kernel(bit, place_ref, mine_ref, got_ref, keep_ref, away_ref):
    low = (place_ref[0] // bit) % 2 == 0
    for d in range(bit):
        a = mine_ref[d] + got_ref[d].astype(jnp.float32)
        b = mine_ref[d + bit] + got_ref[d + bit].astype(jnp.float32)
        keep_ref[d] = jnp.where(low, a, b)
        away_ref[d] = jnp.where(low, b, a).astype(away_ref.dtype)


def add_kernel(*refs):
    out_ref = refs[-1]
    half = refs[0].shape[1]
    for i in range(len(refs) // 2):
        total = refs[2 * i][0] + refs[2 * i + 1][0].astype(jnp.float32)
        out_ref[i * half : (i + 1) * half] = total.astype(out_ref.dtype)


def output_kernel(counts, place_ref, *refs):
    out_ref = refs[-1]
    x = place_ref[3]
    rows = out_ref.shape[0]
    cols = refs[0].shape[1]
    half = rows // 2

    def rows_of(dx, span):
        first = sum(counts[:dx])
        if counts[dx] == 2:
            return refs[first + span][...]
        return refs[first][span * half : (span + 1) * half]

    for at in range(len(counts)):
        for span in range(2):
            block = rows_of(0, span)
            for dx in range(1, len(counts)):
                block = jnp.where((x ^ at) == dx, rows_of(dx, span), block)
            out_ref[span * half : (span + 1) * half, at * cols : (at + 1) * cols] = block


def whole():
    return pl.BlockSpec(memory_space=pltpu.VMEM)


def call(kernel, outs, args, smem=0, scratch=(), vmem=16, flops=0, exps=0):
    several = isinstance(outs, list)
    outs = outs if several else [outs]
    shapes = [jax.ShapeDtypeStruct(shape, kind) for shape, kind in outs]
    moved = sum(a.size * a.dtype.itemsize for a in [*args, *shapes])
    result = pl.pallas_call(
        kernel,
        out_shape=shapes,
        in_specs=[pl.BlockSpec(memory_space=pltpu.SMEM)] * smem + [whole()] * (len(args) - smem),
        out_specs=[whole()] * len(shapes),
        scratch_shapes=list(scratch),
        compiler_params=pltpu.CompilerParams(vmem_limit_bytes=vmem * MIB),
        cost_estimate=pl.CostEstimate(flops=flops, bytes_accessed=moved, transcendentals=exps),
    )(*args)
    return result if several else result[0]


def local(ctx_n, head_n, q_nope, q_rope, latent, k_rope, span_order, w_uk, w_uv, w_o):
    rows = q_nope.shape[0]
    half = rows // 2
    heads = w_uk.shape[1] // NOPE
    depth, cols = w_o.shape
    scale = 1.0 / math.sqrt(NOPE + ROPE)
    xs = head_n // 2
    zs = ctx_n // xs
    zl = zs // 2
    c = lax.axis_index("ctx")
    h = lax.axis_index("head")
    k, y, z, x = h % 2, h // 2, c // xs, c % xs
    place = jnp.stack([c, k, z, x, y, y ^ (zl - 1)]).astype(jnp.int32)
    bf16, f32 = jnp.bfloat16, jnp.float32

    def send(value, where):
        pairs = []
        for ci in range(ctx_n):
            for hi in range(head_n):
                to = where(ci // xs, ci % xs, hi // 2, hi % 2)
                if to is not None:
                    tz, tx, ty, tk = to
                    pairs.append((ci * head_n + hi, (tz * xs + tx) * head_n + ty * 2 + tk))
        return lax.ppermute(value, AXES, pairs)

    keys = call(key_kernel, ((rows, LAT + ROPE), bf16), (latent, k_rope.T), vmem=60)
    pairs = [(d, d + 1) for d in range(1, ctx_n - 1, 2)] + [(None, ctx_n - 1)]

    def across(pair):
        def where(z, x, y, k):
            d = pair[k]
            return None if d is None else (z ^ (d // xs), x ^ (d % xs), y, k)

        return where

    def to_other(pair):
        return lambda z, x, y, k: (z, x, y, 1 - k) if pair[k] is not None else None

    ring = [0, *range(1, zs, 2), *range(zs - 2, 0, -2)]
    following = {z: ring[(i + 1) % zs] for i, z in enumerate(ring)}

    direct = []
    for pair in pairs:
        direct.append(send(keys, across(pair)))
    matrices = [w_o] + [
        send(w_o, lambda z, x, y, k: (z, x ^ dx, y, k)) for dx in range(1, xs)
    ]
    queries = call(
        query_kernel,
        ((heads, rows, LAT + ROPE), bf16),
        (q_nope, q_rope, w_uk),
        vmem=60,
        flops=2 * rows * heads * NOPE * LAT,
    )
    first = len(pairs) // 2
    direct[:first], queries = lax.optimization_barrier((direct[:first], queries))
    passed = [send(direct[i], to_other(pairs[i])) for i in range(first)]
    n_early = 1 + 2 * first
    n_late = ctx_n - n_early

    def work(queries_n, keys_n):
        return 2 * queries_n * heads * keys_n * (2 * LAT + ROPE)

    early = call(
        functools.partial(early_kernel, pairs[:first], 2, scale),
        ((heads, rows, LAT + 128), f32),
        (span_order, place, queries, keys, *direct[:first], *passed[:first]),
        smem=2,
        scratch=(pltpu.VMEM((n_early * rows, LAT + ROPE), bf16),),
        vmem=32,
        flops=work(rows, n_early * rows),
        exps=rows * heads * n_early * rows,
    )
    direct[first:], early = lax.optimization_barrier((direct[first:], early))
    passed += [send(direct[i], to_other(pairs[i])) for i in range(first, len(pairs))]
    blocks = []
    for span in range(2):
        heads_out = call(
            functools.partial(late_kernel, pairs[first:], 4, scale, span),
            ((half, heads * VDIM), bf16),
            (span_order, place, queries, w_uv, early, *direct[first:], *passed[first:]),
            smem=2,
            scratch=(pltpu.VMEM((n_late * rows, LAT + ROPE), bf16),),
            vmem=32,
            flops=work(half, n_late * rows) + 2 * half * heads * LAT * VDIM,
            exps=half * heads * n_late * rows,
        )
        along = [heads_out]
        for _ in range(1, zs):
            along.append(send(along[-1], lambda z, x, y, k: (following[z], x, y, k)))
        blocks.append(along)

    results = []
    counts = COUNTS[0] * (xs - 1) + COUNTS[1]
    sums = {}
    for dx, count in enumerate(counts):
        for span in range(2):
            flip = (dx + span * (count - 1)) % 2 * (zl - 1)
            owner = (y ^ flip).reshape(1).astype(jnp.int32)
            mine, away = call(
                functools.partial(project_kernel, zs),
                [((zl, half, cols), f32), ((zl, half, cols), bf16)],
                (place, matrices[dx], *blocks[span]),
                smem=1,
                scratch=(pltpu.VMEM((zs * half, depth), bf16),),
                flops=2 * zs * half * depth * cols,
            )
            got = send(away, lambda z, x, y, k: (z, x, y, 1 - k))
            bit = zl // 2
            while bit:
                shape = (bit, half, cols)
                mine, away = call(
                    functools.partial(halve_kernel, bit),
                    [(shape, f32), (shape, bf16)],
                    (owner, mine, got),
                    smem=1,
                )
                got = send(away, lambda z, x, y, k: (z, x, y ^ bit, k))
                bit //= 2
            sums[dx, span] = (mine, got, flip)
    last = mine
    for dx, count in enumerate(counts):
        pieces = [sums[dx, 0][:2], sums[dx, 1][:2]]
        if count == 1:
            pieces = [pieces[0] + pieces[1]]
        for i, piece in enumerate(pieces):
            if dx < xs - 1:
                piece, last = lax.optimization_barrier((piece, last))
            block = call(add_kernel, ((rows // count, cols), bf16), piece)
            flip = sums[dx, i][2]
            results.append(send(block, lambda z, x, y, k: (k * zl + (y ^ flip), x, z // 2, z % 2)))
    return call(
        functools.partial(output_kernel, counts),
        ((rows, xs * cols), bf16),
        (place, *results),
        smem=1,
    )


def solution(mesh):
    placed = (
        P("ctx", "head"),
        P("ctx", "head"),
        P("ctx", None),
        P("ctx", None),
        P(),
        P(None, "head"),
        P(None, "head"),
        P("head", "ctx"),
    )
    ctx_n, head_n = mesh.shape["ctx"], mesh.shape["head"]

    def step(*args):
        return local(ctx_n, head_n, *args)

    return jax.shard_map(
        step, mesh=mesh, in_specs=placed, out_specs=P("ctx", "head"), check_vma=False
    )
```

```python
import functools
import math

import jax
import jax.numpy as jnp
from jax import lax
from jax.experimental import pallas as pl
from jax.experimental.pallas import tpu as pltpu
from jax.sharding import PartitionSpec as P

LAT = 512
ROPE = 64
NOPE = 128
VDIM = 128
AXES = ("ctx", "head")
MIB = 1024 * 1024
NT = (((1,), (1,)), ((), ()))


def key_kernel(latent_ref, rope_ref, out_ref):
    out_ref[:, :LAT] = latent_ref[...]
    out_ref[:, LAT:] = rope_ref[...].T


def query_kernel(q_ref, rope_ref, w_ref, out_ref):
    for h in range(out_ref.shape[0]):
        cols = slice(h * NOPE, (h + 1) * NOPE)
        out_ref[h, :, :LAT] = lax.dot_general(
            q_ref[:, cols], w_ref[:, cols], NT, preferred_element_type=jnp.float32
        ).astype(jnp.bfloat16)
        out_ref[h, :, LAT:] = rope_ref[:, h * ROPE : (h + 1) * ROPE]


def place_keys(pairs, order_ref, place_ref, own_ref, direct, passed, keys):
    rows = direct[0].shape[0]
    half = rows // 2
    c = place_ref[0]
    k = place_ref[1]
    lane = lax.broadcasted_iota(jnp.int32, (1, rows), 1)
    places = []

    def add(distance, value):
        slot = 2 * (c ^ distance)
        first = order_ref[slot] * half
        second = order_ref[slot + 1] * half - half
        at = len(places) * rows
        keys[at : at + rows, :] = value
        places.append(lane + jnp.where(lane < half, first, second))

    if own_ref is not None:
        add(0, own_ref[...])
    for (on_0, on_1), mine, other in zip(pairs, direct, passed):
        if on_0 is None:
            add(on_1, jnp.where(k == 0, other[...], mine[...]))
        else:
            add(jnp.where(k == 0, on_0, on_1), mine[...])
            add(jnp.where(k == 0, on_1, on_0), other[...])
    return jnp.concatenate(places, axis=1)


def early_kernel(pairs, group, scale, order_ref, place_ref, q_ref, own_ref, *refs):
    n = len(pairs)
    out_ref, keys = refs[2 * n :]
    key_place = place_keys(
        pairs, order_ref, place_ref, own_ref, refs[:n], refs[n : 2 * n], keys
    )
    heads, rows, _ = q_ref.shape
    half = rows // 2
    c = place_ref[0]
    row = lax.broadcasted_iota(jnp.int32, (rows, 1), 0)
    first = order_ref[2 * c] * half
    second = order_ref[2 * c + 1] * half - half
    visible = key_place <= row + jnp.where(row < half, first, second)
    lane = lax.broadcasted_iota(jnp.int32, (1, 1, 128), 2)
    for g in range(0, heads, group):
        q = q_ref[g : g + group].reshape(group * rows, LAT + ROPE)
        score = lax.dot_general(q, keys[...], NT, preferred_element_type=jnp.float32)
        score = score.reshape(group, rows, -1) * scale
        score = jnp.where(visible[None], score, -1e30)
        top = jnp.max(score, axis=-1, keepdims=True)
        weight = jnp.exp(score - top)
        total = jnp.sum(weight, axis=-1, keepdims=True)
        weight = weight.astype(jnp.bfloat16).reshape(group * rows, -1)
        accum = jnp.dot(weight, keys[:, :LAT], preferred_element_type=jnp.float32)
        out_ref[g : g + group, :, :LAT] = accum.reshape(group, rows, LAT)
        out_ref[g : g + group, :, LAT:] = jnp.where(lane == 0, top, total)


def late_kernel(pairs, group, scale, span, order_ref, place_ref, q_ref, w_ref, early_ref, *refs):
    n = len(pairs)
    out_ref, keys = refs[2 * n :]
    key_place = place_keys(pairs, order_ref, place_ref, None, refs[:n], refs[n : 2 * n], keys)
    heads, rows, _ = q_ref.shape
    half = rows // 2
    c = place_ref[0]
    row = lax.broadcasted_iota(jnp.int32, (half, 1), 0)
    visible = key_place <= row + order_ref[2 * c + span] * half
    these = slice(span * half, (span + 1) * half)
    for g in range(0, heads, group):
        q = q_ref[g : g + group, these, :].reshape(group * half, LAT + ROPE)
        score = lax.dot_general(q, keys[...], NT, preferred_element_type=jnp.float32)
        score = score.reshape(group, half, -1) * scale
        score = jnp.where(visible[None], score, -1e30)
        old = early_ref[g : g + group, these, LAT : LAT + 1]
        total = early_ref[g : g + group, these, LAT + 1 : LAT + 2]
        top = jnp.maximum(old, jnp.max(score, axis=-1, keepdims=True))
        fade = jnp.exp(old - top)
        weight = jnp.exp(score - top)
        total = total * fade + jnp.sum(weight, axis=-1, keepdims=True)
        weight = weight.astype(jnp.bfloat16).reshape(group * half, -1)
        accum = jnp.dot(weight, keys[:, :LAT], preferred_element_type=jnp.float32)
        accum = accum.reshape(group, half, LAT) + early_ref[g : g + group, these, :LAT] * fade
        context = (accum / total).astype(jnp.bfloat16)
        for i in range(group):
            cols = slice((g + i) * VDIM, (g + i + 1) * VDIM)
            out_ref[:, cols] = jnp.dot(
                context[i], w_ref[:, cols], preferred_element_type=jnp.float32
            ).astype(jnp.bfloat16)


def ring_place(z, zs):
    return jnp.where(z % 2 == 1, (z + 1) // 2, (zs - z // 2) % zs)


def ring_member(at, zs):
    return jnp.where(at > zs // 2, 2 * (zs - at), jnp.maximum(2 * at - 1, 0))


def project_kernel(zs, place_ref, w_ref, *refs):
    blocks, mine_ref, away_ref, tokens = refs[:zs], refs[zs], refs[zs + 1], refs[zs + 2]
    zl = zs // 2
    k = place_ref[1]
    half = blocks[0].shape[0]
    for step, block in enumerate(blocks):
        member = ring_member((ring_place(place_ref[2], zs) + zs - step) % zs, zs)
        at = jnp.where(member // zl == k, 0, zl) + member % zl
        tokens[pl.ds(pl.multiple_of(at * half, half), half), :] = block[...]
    part = jnp.dot(tokens[...], w_ref[...], preferred_element_type=jnp.float32)
    part = part.reshape(zs, half, -1)
    mine_ref[...] = part[:zl]
    away_ref[...] = part[zl:].astype(away_ref.dtype)


def halve_kernel(bit, place_ref, mine_ref, got_ref, keep_ref, away_ref):
    low = (place_ref[0] // bit) % 2 == 0
    for d in range(bit):
        a = mine_ref[d] + got_ref[d].astype(jnp.float32)
        b = mine_ref[d + bit] + got_ref[d + bit].astype(jnp.float32)
        keep_ref[d] = jnp.where(low, a, b)
        away_ref[d] = jnp.where(low, b, a).astype(away_ref.dtype)


def add_kernel(*refs):
    out_ref = refs[-1]
    half = refs[0].shape[1]
    for i in range(len(refs) // 2):
        total = refs[2 * i][0] + refs[2 * i + 1][0].astype(jnp.float32)
        out_ref[i * half : (i + 1) * half] = total.astype(out_ref.dtype)


def whole():
    return pl.BlockSpec(memory_space=pltpu.VMEM)


def call(kernel, outs, args, smem=0, scratch=(), vmem=16, flops=0, exps=0):
    several = isinstance(outs, list)
    outs = outs if several else [outs]
    shapes = [jax.ShapeDtypeStruct(shape, kind) for shape, kind in outs]
    moved = sum(a.size * a.dtype.itemsize for a in [*args, *shapes])
    result = pl.pallas_call(
        kernel,
        out_shape=shapes,
        in_specs=[pl.BlockSpec(memory_space=pltpu.SMEM)] * smem + [whole()] * (len(args) - smem),
        out_specs=[whole()] * len(shapes),
        scratch_shapes=list(scratch),
        compiler_params=pltpu.CompilerParams(vmem_limit_bytes=vmem * MIB),
        cost_estimate=pl.CostEstimate(flops=flops, bytes_accessed=moved, transcendentals=exps),
    )(*args)
    return result if several else result[0]


def local(ctx_n, head_n, q_nope, q_rope, latent, k_rope, span_order, w_uk, w_uv, w_o):
    rows = q_nope.shape[0]
    half = rows // 2
    heads = w_uk.shape[1] // NOPE
    depth, cols = w_o.shape
    scale = 1.0 / math.sqrt(NOPE + ROPE)
    xs = head_n // 2
    zs = ctx_n // xs
    zl = zs // 2
    c = lax.axis_index("ctx")
    h = lax.axis_index("head")
    k, y, z, x = h % 2, h // 2, c // xs, c % xs
    place = jnp.stack([c, k, z, x, y, y ^ (zl - 1)]).astype(jnp.int32)
    bf16, f32 = jnp.bfloat16, jnp.float32

    def send(value, where):
        pairs = []
        for ci in range(ctx_n):
            for hi in range(head_n):
                to = where(ci // xs, ci % xs, hi // 2, hi % 2)
                if to is not None:
                    tz, tx, ty, tk = to
                    pairs.append((ci * head_n + hi, (tz * xs + tx) * head_n + ty * 2 + tk))
        return lax.ppermute(value, AXES, pairs)

    keys = call(key_kernel, ((rows, LAT + ROPE), bf16), (latent, k_rope.T), vmem=60)
    pairs = [(d, d + 1) for d in range(1, ctx_n - 1, 2)] + [(None, ctx_n - 1)]

    def across(pair):
        def where(z, x, y, k):
            d = pair[k]
            return None if d is None else (z ^ (d // xs), x ^ (d % xs), y, k)

        return where

    def to_other(pair):
        return lambda z, x, y, k: (z, x, y, 1 - k) if pair[k] is not None else None

    ring = [0, *range(1, zs, 2), *range(zs - 2, 0, -2)]
    following = {z: ring[(i + 1) % zs] for i, z in enumerate(ring)}

    direct = []
    for pair in pairs:
        direct.append(send(keys, across(pair)))
    matrices = [w_o] + [
        send(w_o, lambda z, x, y, k: (z, x ^ dx, y, k)) for dx in range(1, xs)
    ]
    queries = call(
        query_kernel,
        ((heads, rows, LAT + ROPE), bf16),
        (q_nope, q_rope, w_uk),
        vmem=60,
        flops=2 * rows * heads * NOPE * LAT,
    )
    first = len(pairs) // 2
    direct[:first], queries = lax.optimization_barrier((direct[:first], queries))
    passed = [send(direct[i], to_other(pairs[i])) for i in range(first)]
    n_early = 1 + 2 * first
    n_late = ctx_n - n_early

    def work(queries_n, keys_n):
        return 2 * queries_n * heads * keys_n * (2 * LAT + ROPE)

    early = call(
        functools.partial(early_kernel, pairs[:first], 4, scale),
        ((heads, rows, LAT + 128), f32),
        (span_order, place, queries, keys, *direct[:first], *passed[:first]),
        smem=2,
        scratch=(pltpu.VMEM((n_early * rows, LAT + ROPE), bf16),),
        vmem=32,
        flops=work(rows, n_early * rows),
        exps=rows * heads * n_early * rows,
    )
    for i in range(first, len(pairs)):
        direct[i], early = lax.optimization_barrier((direct[i], early))
        passed.append(send(direct[i], to_other(pairs[i])))
    blocks = []
    for span in range(2):
        heads_out = call(
            functools.partial(late_kernel, pairs[first:], 4, scale, span),
            ((half, heads * VDIM), bf16),
            (span_order, place, queries, w_uv, early, *direct[first:], *passed[first:]),
            smem=2,
            scratch=(pltpu.VMEM((n_late * rows, LAT + ROPE), bf16),),
            vmem=32,
            flops=work(half, n_late * rows) + 2 * half * heads * LAT * VDIM,
            exps=half * heads * n_late * rows,
        )
        along = [heads_out]
        for _ in range(1, zs):
            along.append(send(along[-1], lambda z, x, y, k: (following[z], x, y, k)))
        blocks.append(along)

    results = []
    counts = [1] * xs
    sums = {}
    for dx, count in enumerate(counts):
        for span in range(2):
            flip = (dx + span * (count - 1)) % 2 * (zl - 1)
            owner = (y ^ flip).reshape(1).astype(jnp.int32)
            mine, away = call(
                functools.partial(project_kernel, zs),
                [((zl, half, cols), f32), ((zl, half, cols), bf16)],
                (place, matrices[dx], *blocks[span]),
                smem=1,
                scratch=(pltpu.VMEM((zs * half, depth), bf16),),
                flops=2 * zs * half * depth * cols,
            )
            got = send(away, lambda z, x, y, k: (z, x, y, 1 - k))
            bit = zl // 2
            while bit:
                shape = (bit, half, cols)
                mine, away = call(
                    functools.partial(halve_kernel, bit),
                    [(shape, f32), (shape, bf16)],
                    (owner, mine, got),
                    smem=1,
                )
                got = send(away, lambda z, x, y, k: (z, x, y ^ bit, k))
                bit //= 2
            sums[dx, span] = (mine, got, flip)
    last = mine
    for dx, count in enumerate(counts):
        pieces = [sums[dx, 0][:2], sums[dx, 1][:2]]
        if count == 1:
            pieces = [pieces[0] + pieces[1]]
        for i, piece in enumerate(pieces):
            if dx < xs - 1:
                piece, last = lax.optimization_barrier((piece, last))
            block = call(add_kernel, ((rows // count, cols), bf16), piece)
            flip = sums[dx, i][2]
            results.append(send(block, lambda z, x, y, k: (k * zl + (y ^ flip), x, z // 2, z % 2)))
    columns = []
    for at in range(xs):
        block = results[0]
        for dx in range(1, xs):
            block = jnp.where((x ^ at) == dx, results[dx], block)
        columns.append(block)
    return jnp.concatenate(columns, axis=1)


def solution(mesh):
    placed = (
        P("ctx", "head"),
        P("ctx", "head"),
        P("ctx", None),
        P("ctx", None),
        P(),
        P(None, "head"),
        P(None, "head"),
        P("head", "ctx"),
    )
    ctx_n, head_n = mesh.shape["ctx"], mesh.shape["head"]

    def step(*args):
        return local(ctx_n, head_n, *args)

    return jax.shard_map(
        step, mesh=mesh, in_specs=placed, out_specs=P("ctx", "head"), check_vma=False
    )
```

```python
import functools
import math

import jax
import jax.numpy as jnp
from jax import lax
from jax.experimental import pallas as pl
from jax.experimental.pallas import tpu as pltpu
from jax.sharding import PartitionSpec as P

LAT = 512
ROPE = 64
NOPE = 128
VDIM = 128
AXES = ("ctx", "head")
MIB = 1024 * 1024
NT = (((1,), (1,)), ((), ()))


def key_kernel(latent_ref, rope_ref, out_ref):
    out_ref[:, :LAT] = latent_ref[...]
    out_ref[:, LAT:] = rope_ref[...].T


def query_kernel(q_ref, rope_ref, w_ref, out_ref):
    for h in range(out_ref.shape[0]):
        cols = slice(h * NOPE, (h + 1) * NOPE)
        out_ref[h, :, :LAT] = lax.dot_general(
            q_ref[:, cols], w_ref[:, cols], NT, preferred_element_type=jnp.float32
        ).astype(jnp.bfloat16)
        out_ref[h, :, LAT:] = rope_ref[:, h * ROPE : (h + 1) * ROPE]


def place_keys(pairs, order_ref, place_ref, own_ref, direct, passed, keys):
    rows = direct[0].shape[0]
    half = rows // 2
    c = place_ref[0]
    k = place_ref[1]
    lane = lax.broadcasted_iota(jnp.int32, (1, rows), 1)
    places = []

    def add(distance, value):
        slot = 2 * (c ^ distance)
        first = order_ref[slot] * half
        second = order_ref[slot + 1] * half - half
        at = len(places) * rows
        keys[at : at + rows, :] = value
        places.append(lane + jnp.where(lane < half, first, second))

    if own_ref is not None:
        add(0, own_ref[...])
    for (on_0, on_1), mine, other in zip(pairs, direct, passed):
        if on_0 is None:
            add(on_1, jnp.where(k == 0, other[...], mine[...]))
        else:
            add(jnp.where(k == 0, on_0, on_1), mine[...])
            add(jnp.where(k == 0, on_1, on_0), other[...])
    return jnp.concatenate(places, axis=1)


def early_kernel(pairs, group, scale, order_ref, place_ref, q_ref, own_ref, *refs):
    n = len(pairs)
    out_ref, keys = refs[2 * n :]
    key_place = place_keys(
        pairs, order_ref, place_ref, own_ref, refs[:n], refs[n : 2 * n], keys
    )
    heads, rows, _ = q_ref.shape
    half = rows // 2
    c = place_ref[0]
    row = lax.broadcasted_iota(jnp.int32, (rows, 1), 0)
    first = order_ref[2 * c] * half
    second = order_ref[2 * c + 1] * half - half
    visible = key_place <= row + jnp.where(row < half, first, second)
    lane = lax.broadcasted_iota(jnp.int32, (1, 1, 128), 2)
    for g in range(0, heads, group):
        q = q_ref[g : g + group].reshape(group * rows, LAT + ROPE)
        score = lax.dot_general(q, keys[...], NT, preferred_element_type=jnp.float32)
        score = score.reshape(group, rows, -1) * scale
        score = jnp.where(visible[None], score, -1e30)
        top = jnp.max(score, axis=-1, keepdims=True)
        weight = jnp.exp(score - top)
        total = jnp.sum(weight, axis=-1, keepdims=True)
        weight = weight.astype(jnp.bfloat16).reshape(group * rows, -1)
        accum = jnp.dot(weight, keys[:, :LAT], preferred_element_type=jnp.float32)
        out_ref[g : g + group, :, :LAT] = accum.reshape(group, rows, LAT)
        out_ref[g : g + group, :, LAT:] = jnp.where(lane == 0, top, total)


def late_kernel(pairs, group, scale, span, order_ref, place_ref, q_ref, w_ref, early_ref, *refs):
    n = len(pairs)
    out_ref, keys = refs[2 * n :]
    key_place = place_keys(pairs, order_ref, place_ref, None, refs[:n], refs[n : 2 * n], keys)
    heads, rows, _ = q_ref.shape
    half = rows // 2
    c = place_ref[0]
    row = lax.broadcasted_iota(jnp.int32, (half, 1), 0)
    visible = key_place <= row + order_ref[2 * c + span] * half
    these = slice(span * half, (span + 1) * half)
    for g in range(0, heads, group):
        q = q_ref[g : g + group, these, :].reshape(group * half, LAT + ROPE)
        score = lax.dot_general(q, keys[...], NT, preferred_element_type=jnp.float32)
        score = score.reshape(group, half, -1) * scale
        score = jnp.where(visible[None], score, -1e30)
        old = early_ref[g : g + group, these, LAT : LAT + 1]
        total = early_ref[g : g + group, these, LAT + 1 : LAT + 2]
        top = jnp.maximum(old, jnp.max(score, axis=-1, keepdims=True))
        fade = jnp.exp(old - top)
        weight = jnp.exp(score - top)
        total = total * fade + jnp.sum(weight, axis=-1, keepdims=True)
        weight = weight.astype(jnp.bfloat16).reshape(group * half, -1)
        accum = jnp.dot(weight, keys[:, :LAT], preferred_element_type=jnp.float32)
        accum = accum.reshape(group, half, LAT) + early_ref[g : g + group, these, :LAT] * fade
        context = (accum / total).astype(jnp.bfloat16)
        for i in range(group):
            cols = slice((g + i) * VDIM, (g + i + 1) * VDIM)
            out_ref[:, cols] = jnp.dot(
                context[i], w_ref[:, cols], preferred_element_type=jnp.float32
            ).astype(jnp.bfloat16)


def ring_place(z, zs):
    return jnp.where(z % 2 == 1, (z + 1) // 2, (zs - z // 2) % zs)


def ring_member(at, zs):
    return jnp.where(at > zs // 2, 2 * (zs - at), jnp.maximum(2 * at - 1, 0))


def project_kernel(zs, place_ref, w_ref, *refs):
    blocks, mine_ref, away_ref, tokens = refs[:zs], refs[zs], refs[zs + 1], refs[zs + 2]
    zl = zs // 2
    k = place_ref[1]
    half = blocks[0].shape[0]
    for step, block in enumerate(blocks):
        member = ring_member((ring_place(place_ref[2], zs) + zs - step) % zs, zs)
        distance = member ^ place_ref[2]
        at = jnp.where(distance // zl == k, 0, zl) + distance % zl
        tokens[pl.ds(pl.multiple_of(at * half, half), half), :] = block[...]
    part = jnp.dot(tokens[...], w_ref[...], preferred_element_type=jnp.float32)
    part = part.reshape(zs, half, -1)
    mine_ref[...] = part[:zl]
    away_ref[...] = part[zl:].astype(away_ref.dtype)


def halve_kernel(bit, place_ref, mine_ref, got_ref, keep_ref, away_ref):
    low = (place_ref[0] // bit) % 2 == 0
    for d in range(bit):
        a = mine_ref[d] + got_ref[d].astype(jnp.float32)
        b = mine_ref[d + bit] + got_ref[d + bit].astype(jnp.float32)
        keep_ref[d] = jnp.where(low, a, b)
        away_ref[d] = jnp.where(low, b, a).astype(away_ref.dtype)


def add_kernel(*refs):
    out_ref = refs[-1]
    half = refs[0].shape[1]
    for i in range(len(refs) // 2):
        total = refs[2 * i][0] + refs[2 * i + 1][0].astype(jnp.float32)
        out_ref[i * half : (i + 1) * half] = total.astype(out_ref.dtype)


def whole():
    return pl.BlockSpec(memory_space=pltpu.VMEM)


def call(kernel, outs, args, smem=0, scratch=(), vmem=16, flops=0, exps=0):
    several = isinstance(outs, list)
    outs = outs if several else [outs]
    shapes = [jax.ShapeDtypeStruct(shape, kind) for shape, kind in outs]
    moved = sum(a.size * a.dtype.itemsize for a in [*args, *shapes])
    result = pl.pallas_call(
        kernel,
        out_shape=shapes,
        in_specs=[pl.BlockSpec(memory_space=pltpu.SMEM)] * smem + [whole()] * (len(args) - smem),
        out_specs=[whole()] * len(shapes),
        scratch_shapes=list(scratch),
        compiler_params=pltpu.CompilerParams(vmem_limit_bytes=vmem * MIB),
        cost_estimate=pl.CostEstimate(flops=flops, bytes_accessed=moved, transcendentals=exps),
    )(*args)
    return result if several else result[0]


def local(ctx_n, head_n, q_nope, q_rope, latent, k_rope, span_order, w_uk, w_uv, w_o):
    rows = q_nope.shape[0]
    half = rows // 2
    heads = w_uk.shape[1] // NOPE
    depth, cols = w_o.shape
    scale = 1.0 / math.sqrt(NOPE + ROPE)
    xs = head_n // 2
    zs = ctx_n // xs
    zl = zs // 2
    c = lax.axis_index("ctx")
    h = lax.axis_index("head")
    k, y, z, x = h % 2, h // 2, c // xs, c % xs
    place = jnp.stack([c, k, z, x, y, y ^ (zl - 1)]).astype(jnp.int32)
    bf16, f32 = jnp.bfloat16, jnp.float32

    def send(value, where):
        pairs = []
        for ci in range(ctx_n):
            for hi in range(head_n):
                to = where(ci // xs, ci % xs, hi // 2, hi % 2)
                if to is not None:
                    tz, tx, ty, tk = to
                    pairs.append((ci * head_n + hi, (tz * xs + tx) * head_n + ty * 2 + tk))
        return lax.ppermute(value, AXES, pairs)

    keys = call(key_kernel, ((rows, LAT + ROPE), bf16), (latent, k_rope.T), vmem=60)
    pairs = [(d, d + 1) for d in range(1, ctx_n - 1, 2)] + [(None, ctx_n - 1)]

    def across(pair):
        def where(z, x, y, k):
            d = pair[k]
            return None if d is None else (z ^ (d // xs), x ^ (d % xs), y, k)

        return where

    def to_other(pair):
        return lambda z, x, y, k: (z, x, y, 1 - k) if pair[k] is not None else None

    ring = [0, *range(1, zs, 2), *range(zs - 2, 0, -2)]
    following = {z: ring[(i + 1) % zs] for i, z in enumerate(ring)}

    direct = []
    for pair in pairs:
        direct.append(send(keys, across(pair)))
    matrices = [w_o] + [
        send(w_o, lambda z, x, y, k: (z, x ^ dx, y, k)) for dx in range(1, xs)
    ]
    queries = call(
        query_kernel,
        ((heads, rows, LAT + ROPE), bf16),
        (q_nope, q_rope, w_uk),
        vmem=60,
        flops=2 * rows * heads * NOPE * LAT,
    )
    first = len(pairs) // 2
    direct[:first], queries = lax.optimization_barrier((direct[:first], queries))
    passed = [send(direct[i], to_other(pairs[i])) for i in range(first)]
    n_early = 1 + 2 * first
    n_late = ctx_n - n_early

    def work(queries_n, keys_n):
        return 2 * queries_n * heads * keys_n * (2 * LAT + ROPE)

    early = call(
        functools.partial(early_kernel, pairs[:first], 4, scale),
        ((heads, rows, LAT + 128), f32),
        (span_order, place, queries, keys, *direct[:first], *passed[:first]),
        smem=2,
        scratch=(pltpu.VMEM((n_early * rows, LAT + ROPE), bf16),),
        vmem=32,
        flops=work(rows, n_early * rows),
        exps=rows * heads * n_early * rows,
    )
    for i in range(first, len(pairs)):
        direct[i], early = lax.optimization_barrier((direct[i], early))
        passed.append(send(direct[i], to_other(pairs[i])))
    blocks = []
    for span in range(2):
        heads_out = call(
            functools.partial(late_kernel, pairs[first:], 4, scale, span),
            ((half, heads * VDIM), bf16),
            (span_order, place, queries, w_uv, early, *direct[first:], *passed[first:]),
            smem=2,
            scratch=(pltpu.VMEM((n_late * rows, LAT + ROPE), bf16),),
            vmem=32,
            flops=work(half, n_late * rows) + 2 * half * heads * LAT * VDIM,
            exps=half * heads * n_late * rows,
        )
        along = [heads_out]
        for _ in range(1, zs):
            along.append(send(along[-1], lambda z, x, y, k: (following[z], x, y, k)))
        blocks.append(along)

    results = []
    counts = [1] * xs
    sums = {}
    for dx, count in enumerate(counts):
        for span in range(2):
            flip = (dx + span * (count - 1)) % 2 * (zl - 1)
            owner = (y ^ flip).reshape(1).astype(jnp.int32)
            mine, away = call(
                functools.partial(project_kernel, zs),
                [((zl, half, cols), f32), ((zl, half, cols), bf16)],
                (place, matrices[dx], *blocks[span]),
                smem=1,
                scratch=(pltpu.VMEM((zs * half, depth), bf16),),
                flops=2 * zs * half * depth * cols,
            )
            got = send(away, lambda z, x, y, k: (z, x, y, 1 - k))
            bit = zl // 2
            while bit:
                shape = (bit, half, cols)
                mine, away = call(
                    functools.partial(halve_kernel, bit),
                    [(shape, f32), (shape, bf16)],
                    (owner, mine, got),
                    smem=1,
                )
                got = send(away, lambda z, x, y, k: (z, x, y ^ bit, k))
                bit //= 2
            sums[dx, span] = (mine, got, flip)
    last = mine
    for dx, count in enumerate(counts):
        pieces = [sums[dx, 0][:2], sums[dx, 1][:2]]
        if count == 1:
            pieces = [pieces[0] + pieces[1]]
        for i, piece in enumerate(pieces):
            if dx < xs - 1:
                piece, last = lax.optimization_barrier((piece, last))
            block = call(add_kernel, ((rows // count, cols), bf16), piece)
            flip = sums[dx, i][2]
            results.append(
                send(block, lambda z, x, y, k: (z ^ (k * zl + (y ^ flip)), x, z // 2, z % 2))
            )
    columns = []
    for at in range(xs):
        block = results[0]
        for dx in range(1, xs):
            block = jnp.where((x ^ at) == dx, results[dx], block)
        columns.append(block)
    return jnp.concatenate(columns, axis=1)


def solution(mesh):
    placed = (
        P("ctx", "head"),
        P("ctx", "head"),
        P("ctx", None),
        P("ctx", None),
        P(),
        P(None, "head"),
        P(None, "head"),
        P("head", "ctx"),
    )
    ctx_n, head_n = mesh.shape["ctx"], mesh.shape["head"]

    def step(*args):
        return local(ctx_n, head_n, *args)

    return jax.shard_map(
        step, mesh=mesh, in_specs=placed, out_specs=P("ctx", "head"), check_vma=False
    )
```
